32 devices in a mesh: rep: 2 (over x), exp: 16 (over z, y, core).
Axes of the slice: x: 2, y: 2, z: 4, core: 2. Of those that a mesh axis runs over, the one named last changes fastest.
Arguments:
- tokens: bfloat16 [2, 2048, 2048], P('rep', 'exp'), may hold values from -6 to 6
- cotangent: bfloat16 [2, 2048, 2048], P('rep', 'exp'), may hold values from -6 to 6
- routes: int32 [2, 2048, 8], P('rep', 'exp'), may hold values from 0 to 15, all different within a row; in each aligned block of 128 rows (0 to 127, 128 to 255, ..., all dimensions but the last counted through in order) at most 96 rows name the same one
- router_pair_weight: bfloat16 [2, 2048, 8], P('rep', 'exp'), may hold values from 0.019897461 to 0.5
- capacity: int32 [16], replicated, may hold values from 512 to 1024, as said below
- training_step_index: int32 [1], replicated, may hold values from 0 to 999
- frozen_gate_matrix: bfloat16 [16, 2048, 768], P('exp'), may hold values from -0.125 to 0.125
- frozen_up_matrix: bfloat16 [16, 2048, 768], P('exp'), may hold values from -0.125 to 0.125
- frozen_down_matrix: bfloat16 [16, 768, 2048], P('exp'), may hold values from -0.21875 to 0.21875
- adapter_input_factor: float32 [2, 16, 16, 768], P('rep', 'exp'), may hold values from -0.6 to 0.6
- adapter_output_factor: float32 [2, 16, 16, 2048], P('rep', 'exp'), may hold values from -1.5 to 1.5
- input_first_moment: float32 [2, 16, 16, 768], P('rep', 'exp'), may hold values from -2 to 2
- output_first_moment: float32 [2, 16, 16, 2048], P('rep', 'exp'), may hold values from -2 to 2
- input_second_moment: float32 [2, 16, 16, 768], P('rep', 'exp'), may hold values from 0.05 to 5
- output_second_moment: float32 [2, 16, 16, 2048], P('rep', 'exp'), may hold values from 0.05 to 5
Outputs:
- combined: bfloat16 [2, 2048, 2048], P('rep', 'exp')
- new_lora_in: float32 [2, 16, 16, 768], P('rep', 'exp')
- new_lora_out: float32 [2, 16, 16, 2048], P('rep', 'exp')
- new_first_in: float32 [2, 16, 16, 768], P('rep', 'exp')
- new_first_out: float32 [2, 16, 16, 2048], P('rep', 'exp')
- new_second_in: float32 [2, 16, 16, 768], P('rep', 'exp')
- new_second_out: float32 [2, 16, 16, 2048], P('rep', 'exp')
The draws below stay inside these ranges and needn't reach their ends.
Inputs may be any that keep to these rules, and one draw needn't show every extreme that they name: `routes`: in the rows of one device, no expert is named more than 96 times; a token names distinct experts. The largest capacity is exactly 1024.
All inputs are finite; a program needn't handle non-finite values.
Results may differ from the reference program's by a relative error of at most 0.007.
Values may be sent and summed in bfloat16 or wider, within the bound.
A program may use at most 128 MiB of HBM per device.

```python
import math
import jax
import jax.numpy as jnp
import numpy as np
from jax import lax

HIDDEN_WIDTH = 2048
EXPERT_UNITS = 768
ADAPTER_RANK = 16
TOP = 8
TOK_DEV = 128
REPLICA_COUNT = 2
TOKENS = 2048
WINDOW_EXPERTS = 16
MOST = 96
CAP_MOST = 1024
N_REP = 2


def draw_capacity(key, part):
    first_key, second_key = jax.random.split(jax.random.fold_in(key, 17))
    drawn = jax.random.randint(first_key, (WINDOW_EXPERTS,), CAP_MOST // 2, CAP_MOST + 1)
    chosen = jax.random.randint(second_key, (), 0, WINDOW_EXPERTS)
    return jnp.where(jnp.arange(WINDOW_EXPERTS) == chosen, CAP_MOST, drawn).astype(jnp.int32)


def block_scale(rng, dims, cuts, least, largest):
    factor_of, own = 1.0, jax.random.fold_in(rng, 6)
    for axis_at, parts in cuts:
        steps = jnp.exp(jax.random.uniform(jax.random.fold_in(own, axis_at), (parts,), jnp.float32, least / len(cuts), largest / len(cuts)))
        factor_of = factor_of * jnp.repeat(steps, dims[axis_at] // parts).reshape([-1 if axis == axis_at else 1 for axis in range(len(dims))])
    return factor_of


def routed_block(rng, own, number, rows, count, top, bound, lean):
    sequence = jax.random.permutation(rng, count)
    crowded, ordinary = load_shares(count, rows * top, bound, lean, True), load_shares(count, rows * top, bound, lean, False)
    places = jnp.arange(count)

    def named(tallies, rotation):
        used = int((tallies > 0).sum())
        fixed = max(1, used // 4)
        shifted = fixed + (places - fixed + rotation * (used - fixed)) % max(1, count - fixed)
        return jnp.zeros((count,), jnp.int32).at[sequence[jnp.where(places < fixed, places, shifted)]].set(jnp.asarray(tallies, jnp.int32))

    tallies = jnp.where(number % 4 == 0, named(crowded, number // 4), named(ordinary, number - number // 4 - 1))
    mixed = jax.random.permutation(jax.random.fold_in(own, 3), count)
    giver, receiver = mixed[0:count // 2 * 2:2], mixed[1:count // 2 * 2:2]
    slack = jnp.minimum(tallies[giver] - 1, bound - tallies[receiver]) // 2
    slack = jnp.where((giver == sequence[0]) | (receiver == sequence[0]) | (tallies[receiver] == 0), 0, jnp.maximum(slack, 0))
    shifted = jax.random.randint(jax.random.fold_in(own, 4), (count // 2,), 0, 1 << 20) % (slack + 1)
    tallies = tallies.at[giver].add(-shifted).at[receiver].add(shifted)
    labels = jnp.searchsorted(jnp.cumsum(tallies), jnp.arange(rows * top), side="right").astype(jnp.int32)
    grid = labels.reshape(top, rows).T
    grid = grid[jax.random.permutation(jax.random.fold_in(own, 1), rows)]
    rotation = jax.random.randint(jax.random.fold_in(own, 2), (rows, 1), 0, top)
    return jnp.take_along_axis(grid, (jnp.arange(top)[None, :] + rotation) % top, axis=1)


def load_shares(number_of, total, reach, skew, full):
    portions = [(1 << 20) // math.isqrt(grade ** skew) + 1 for grade in range(1, number_of + 1)]
    largest = reach if full else min(reach, max(-(-total // number_of), total * portions[0] // sum(portions)))
    least = 1 if total - largest >= number_of - 1 else 0
    holding, surplus = [largest] + [least] * (number_of - 1), total - largest - least * (number_of - 1)
    while surplus > 0:
        free = [i for i in range(1, number_of) if holding[i] < largest] or [i for i in range(1, number_of) if holding[i] < reach]
        pool, left = sum([portions[i] for i in free]), surplus
        for i in free:
            more = min(reach - holding[i], max(1, left * portions[i] // pool), surplus)
            holding[i] = holding[i] + more
            surplus = surplus - more
    return np.array(holding)


def noise(rng, dims, width, reach, cuts=(), kind=jnp.bfloat16):
    result = width * jax.random.normal(rng, dims, jnp.float32)
    if cuts:
        result = result * block_scale(rng, dims, cuts, -0.22, 0.18)
    return jnp.clip(result, -reach, reach).astype(kind)


def setup_inputs(seed: int = 0) -> dict:
    arg_keys = jax.random.split(jax.random.key(seed), 16)
    tokens = noise(arg_keys[0], (REPLICA_COUNT, TOKENS, HIDDEN_WIDTH), 1.0, 6.0, ((0, 2), (1, 16)))
    cotangent = noise(arg_keys[1], (REPLICA_COUNT, TOKENS, HIDDEN_WIDTH), 1.0, 6.0, ((0, 2), (1, 16)))
    routes_keys = jax.random.split(jax.random.fold_in(arg_keys[2], 1), REPLICA_COUNT * TOKENS // TOK_DEV)
    routes_turns = jax.random.permutation(jax.random.fold_in(arg_keys[2], 3), REPLICA_COUNT * TOKENS // TOK_DEV)
    routes = jax.vmap(lambda own, number: routed_block(jax.random.fold_in(arg_keys[2], 2), own, number, TOK_DEV, WINDOW_EXPERTS, TOP, MOST, 2))(routes_keys, routes_turns).reshape((REPLICA_COUNT, TOKENS, TOP))
    router_pair_weight = jnp.clip(jnp.exp(math.log(0.5) - 3.224016 * jax.random.uniform(arg_keys[3], (REPLICA_COUNT, TOKENS, TOP), jnp.float32) ** block_scale(arg_keys[3], (REPLICA_COUNT, TOKENS, TOP), ((0, 2), (1, 16)), -0.2, 0.2)), 0.019897461, 0.5).astype(jnp.bfloat16)
    capacity = draw_capacity(jax.random.fold_in(arg_keys[15], 71), 0)
    training_step_index = jax.random.randint(arg_keys[5], (1,), 0, 1000).astype(jnp.int32)
    frozen_gate_matrix = noise(arg_keys[6], (WINDOW_EXPERTS, HIDDEN_WIDTH, EXPERT_UNITS), HIDDEN_WIDTH ** -0.5, 0.125, ((0, 16),))
    frozen_up_matrix = noise(arg_keys[7], (WINDOW_EXPERTS, HIDDEN_WIDTH, EXPERT_UNITS), HIDDEN_WIDTH ** -0.5, 0.125, ((0, 16),))
    frozen_down_matrix = noise(arg_keys[8], (WINDOW_EXPERTS, EXPERT_UNITS, HIDDEN_WIDTH), EXPERT_UNITS ** -0.5, 0.21875, ((0, 16),))
    adapter_input_factor = noise(arg_keys[9], (REPLICA_COUNT, WINDOW_EXPERTS, ADAPTER_RANK, EXPERT_UNITS), 0.1, 0.6, ((0, 2), (1, 16)), jnp.float32)
    adapter_output_factor = noise(arg_keys[10], (REPLICA_COUNT, WINDOW_EXPERTS, ADAPTER_RANK, HIDDEN_WIDTH), 0.25, 1.5, ((0, 2), (1, 16)), jnp.float32)
    input_first_moment = noise(arg_keys[11], (REPLICA_COUNT, WINDOW_EXPERTS, ADAPTER_RANK, EXPERT_UNITS), 0.3, 2.0, ((0, 2), (1, 16)), jnp.float32)
    output_first_moment = noise(arg_keys[12], (REPLICA_COUNT, WINDOW_EXPERTS, ADAPTER_RANK, HIDDEN_WIDTH), 0.3, 2.0, ((0, 2), (1, 16)), jnp.float32)
    input_second_moment = jnp.clip(jnp.exp(math.log(5.0) - 4.6051702 * jax.random.uniform(arg_keys[13], (REPLICA_COUNT, WINDOW_EXPERTS, ADAPTER_RANK, EXPERT_UNITS), jnp.float32) ** block_scale(arg_keys[13], (REPLICA_COUNT, WINDOW_EXPERTS, ADAPTER_RANK, EXPERT_UNITS), ((0, 2), (1, 16)), -0.2, 0.2)), 0.05, 5.0)
    output_second_moment = jnp.clip(jnp.exp(math.log(5.0) - 4.6051702 * jax.random.uniform(arg_keys[14], (REPLICA_COUNT, WINDOW_EXPERTS, ADAPTER_RANK, HIDDEN_WIDTH), jnp.float32) ** block_scale(arg_keys[14], (REPLICA_COUNT, WINDOW_EXPERTS, ADAPTER_RANK, HIDDEN_WIDTH), ((0, 2), (1, 16)), -0.2, 0.2)), 0.05, 5.0)
    return dict(tokens=tokens, cotangent=cotangent, routes=routes, router_pair_weight=router_pair_weight, capacity=capacity, training_step_index=training_step_index, frozen_gate_matrix=frozen_gate_matrix, frozen_up_matrix=frozen_up_matrix, frozen_down_matrix=frozen_down_matrix, adapter_input_factor=adapter_input_factor, adapter_output_factor=adapter_output_factor, input_first_moment=input_first_moment, output_first_moment=output_first_moment, input_second_moment=input_second_moment, output_second_moment=output_second_moment)


adapter_scale = 0.5
beta_one = 0.9
beta_two = 0.999
learn_rate = 0.02
weight_decay = 0.01
epsilon = 1e-08

def route_ranks(route_rows):
    expert_ids = jnp.arange(WINDOW_EXPERTS, dtype=jnp.int32)
    route_hits = (route_rows[:, :, None] == expert_ids[None, None, :]).astype(jnp.int32)
    per_token = lax.optimization_barrier(jnp.sum(route_hits, axis=1))
    before = jnp.cumsum(per_token, axis=0) - per_token
    return (route_hits, lax.optimization_barrier(jnp.sum(route_hits * before[:, None, :], axis=2)))

def one_replica(item, capacity, frozen_gate_matrix, frozen_up_matrix, frozen_down_matrix):
    token_rows, cot_rows, route_rows, weight_rows, in_rep, out_rep = item
    route_hits, rank_table = route_ranks(route_rows)
    cap_pairs = lax.optimization_barrier(jnp.sum(route_hits * capacity[None, None, :], axis=2))
    kept_mask = rank_table < cap_pairs
    total_slots = WINDOW_EXPERTS * CAP_MOST
    place = jnp.where(kept_mask, route_rows * CAP_MOST + rank_table, total_slots).reshape(-1)
    token_ids = jnp.broadcast_to(jnp.arange(TOKENS, dtype=jnp.int32)[:, None], (TOKENS, TOP)).reshape(-1)
    row_index = jnp.zeros((total_slots,), jnp.int32).at[place].set(token_ids, mode='drop')
    row_valid = jnp.zeros((total_slots,), jnp.float32).at[place].set(1.0, mode='drop')
    row_weight = jnp.zeros((total_slots,), jnp.float32).at[place].set(weight_rows.astype(jnp.float32).reshape(-1), mode='drop')
    input_factor_batch = in_rep.astype(jnp.bfloat16)
    output_factor_batch = out_rep.astype(jnp.bfloat16)

    def one_expert(expert_item):
        slot_index, slot_valid, slot_weight, w_gate, w_up, down_projection_matrix, in_one, single_output_rows = expert_item
        picked = token_rows[slot_index] * slot_valid[:, None].astype(jnp.bfloat16)
        row_gradient_values = (slot_weight[:, None] * cot_rows[slot_index].astype(jnp.float32)).astype(jnp.bfloat16)
        gate = jnp.dot(picked, w_gate, preferred_element_type=jnp.float32)
        upper = jnp.dot(picked, w_up, preferred_element_type=jnp.float32)
        hidden_activation = (jax.nn.silu(gate) * upper).astype(jnp.bfloat16)
        projected_rank_rows = jnp.dot(hidden_activation, in_one.T, preferred_element_type=jnp.float32).astype(jnp.bfloat16)
        expert_result_rows = (jnp.dot(hidden_activation, down_projection_matrix, preferred_element_type=jnp.float32) + adapter_scale * jnp.dot(projected_rank_rows, single_output_rows, preferred_element_type=jnp.float32)).astype(jnp.bfloat16)
        output_factor_gradient = adapter_scale * jnp.dot(projected_rank_rows.T, row_gradient_values, preferred_element_type=jnp.float32)
        returned_rank_rows = jnp.dot(row_gradient_values, single_output_rows.T, preferred_element_type=jnp.float32).astype(jnp.bfloat16)
        input_factor_gradient = adapter_scale * jnp.dot(returned_rank_rows.T, hidden_activation, preferred_element_type=jnp.float32)
        return (expert_result_rows, input_factor_gradient, output_factor_gradient)
    expert_result_rows, input_factor_gradient, output_factor_gradient = lax.map(one_expert, (row_index.reshape(WINDOW_EXPERTS, CAP_MOST), row_valid.reshape(WINDOW_EXPERTS, CAP_MOST), row_weight.reshape(WINDOW_EXPERTS, CAP_MOST), frozen_gate_matrix, frozen_up_matrix, frozen_down_matrix, input_factor_batch, output_factor_batch))
    out_table = expert_result_rows.reshape(total_slots, HIDDEN_WIDTH)
    pick_index = jnp.where(kept_mask, route_rows * CAP_MOST + rank_table, 0)
    summed = jnp.zeros((TOKENS, HIDDEN_WIDTH), jnp.float32)
    for slot_k in range(TOP):
        scale_k = jnp.where(kept_mask[:, slot_k], weight_rows[:, slot_k].astype(jnp.float32), jnp.float32(0.0))
        summed = summed + scale_k[:, None] * out_table[pick_index[:, slot_k]].astype(jnp.float32)
    return (summed.astype(jnp.bfloat16), input_factor_gradient, output_factor_gradient)

def adam_update(averaged, gradient, first_moment, second_moment, fix_one, fix_two):
    new_first = beta_one * first_moment + (1.0 - beta_one) * gradient
    new_second = beta_two * second_moment + (1.0 - beta_two) * gradient * gradient
    stepped = new_first / fix_one / (jnp.sqrt(new_second / fix_two) + epsilon)
    return (averaged - learn_rate * (stepped + weight_decay * averaged), new_first, new_second)

def reference(tokens, cotangent, routes, router_pair_weight, capacity, training_step_index, frozen_gate_matrix, frozen_up_matrix, frozen_down_matrix, adapter_input_factor, adapter_output_factor, input_first_moment, output_first_moment, input_second_moment, output_second_moment):

    def replica_function(item):
        return one_replica(item, capacity, frozen_gate_matrix, frozen_up_matrix, frozen_down_matrix)
    combined, input_factor_gradient, output_factor_gradient = lax.map(replica_function, (tokens, cotangent, routes, router_pair_weight, adapter_input_factor, adapter_output_factor))
    levels = N_REP.bit_length() - 1
    level_bit = (training_step_index[0] % levels).astype(jnp.int32)
    gossip_neighbor = jnp.bitwise_xor(jnp.arange(REPLICA_COUNT, dtype=jnp.int32), jnp.left_shift(jnp.ones((), jnp.int32), level_bit))
    mean_input_factor = 0.5 * (adapter_input_factor + adapter_input_factor[gossip_neighbor])
    mean_output_factor = 0.5 * (adapter_output_factor + adapter_output_factor[gossip_neighbor])
    power = (training_step_index[0] + 1).astype(jnp.float32)
    fix_one = 1.0 - jnp.power(jnp.float32(beta_one), power)
    fix_two = 1.0 - jnp.power(jnp.float32(beta_two), power)
    new_in, new_first_in, new_second_in = adam_update(mean_input_factor, input_factor_gradient, input_first_moment, input_second_moment, fix_one, fix_two)
    new_out, new_first_out, new_second_out = adam_update(mean_output_factor, output_factor_gradient, output_first_moment, output_second_moment, fix_one, fix_two)
    return (combined, new_in, new_out, new_first_in, new_first_out, new_second_in, new_second_out)
```

```python
from functools import partial

import jax
import jax.numpy as jnp
from jax import lax
from jax.sharding import PartitionSpec as P

adapter_scale = 0.5
beta_one = 0.9
beta_two = 0.999
learn_rate = 0.02
weight_decay = 0.01
epsilon = 1e-08


def as_sent(x):
    return jax.tree.map(lambda a: a.astype(jnp.bfloat16) if a.dtype == jnp.float32 else a, x)


def partner(value, axis, stride):
    mask = 2**stride
    pairs = [(source, source ^ mask) for source in range(lax.axis_size(axis))]
    return lax.ppermute(value, axis, pairs)


def swap_with(joined_rows, level_bit):
    return jax.tree.map(
        lambda part, own: part.astype(own.dtype),
        partner(as_sent(joined_rows), "rep", level_bit),
        joined_rows,
    )


def adam_update(averaged, gradient, first_moment, second_moment, fix_one, fix_two):
    new_first = beta_one * first_moment + (1.0 - beta_one) * gradient
    new_second = beta_two * second_moment + (1.0 - beta_two) * gradient * gradient
    stepped = new_first / fix_one / (jnp.sqrt(new_second / fix_two) + epsilon)
    return (averaged - learn_rate * (stepped + weight_decay * averaged), new_first, new_second)


def per_device(
    tokens,
    cotangent,
    routes,
    router_pair_weight,
    capacity,
    training_step_index,
    frozen_gate_matrix,
    frozen_up_matrix,
    frozen_down_matrix,
    adapter_input_factor,
    adapter_output_factor,
    input_first_moment,
    output_first_moment,
    input_second_moment,
    output_second_moment,
):
    devices = lax.axis_size("exp")
    me = lax.axis_index("exp")
    assert frozen_gate_matrix.shape[0] == 1
    tok_dev, width = tokens.shape[1:]
    rank = adapter_output_factor.shape[2]
    own_grads = cotangent[0]
    in_b = adapter_input_factor[0, 0].astype(jnp.bfloat16)
    out_b = adapter_output_factor[0, 0].astype(jnp.bfloat16)

    hits = routes[0][None, :, :] == jnp.arange(devices, dtype=jnp.int32)[:, None, None]
    table = jnp.sum(
        jnp.where(hits, router_pair_weight[0].astype(jnp.float32)[None], 0.0), axis=2
    ).astype(jnp.bfloat16)
    small = jnp.concatenate((out_b, table.reshape(-1, width)), axis=0)
    small_all = lax.all_gather(small, "exp")
    rows_all = lax.all_gather(tokens[0], "exp", tiled=True)

    out_all = small_all[:, :rank].reshape(devices * rank, width)
    table_all = small_all[:, rank:].reshape(devices, devices, tok_dev).astype(jnp.float32)
    hit_all = (table_all > 0).astype(jnp.float32)
    earlier = jnp.triu(jnp.ones((tok_dev, tok_dev), jnp.float32), 1)
    within = jnp.einsum("set,tu->seu", hit_all, earlier)
    counts = jnp.sum(hit_all, axis=2)
    start = jnp.cumsum(counts, axis=0) - counts
    position = start[:, :, None] + within
    kept = position < capacity.astype(jnp.float32)[None, :, None]
    table_all = jnp.where(kept, table_all, 0.0)
    own_table = lax.dynamic_index_in_dim(table_all, me, 0, keepdims=False)
    expert_weight = lax.dynamic_index_in_dim(table_all, me, 1, keepdims=False).reshape(-1)

    back = jnp.einsum("td,cd->tc", own_grads, out_all, preferred_element_type=jnp.float32)
    back = back.reshape(tok_dev, devices, rank).transpose(1, 0, 2) * own_table[:, :, None]
    back = lax.all_to_all(back.astype(jnp.bfloat16), "exp", 0, 0, tiled=True)
    back = back.reshape(devices * tok_dev, rank)

    gate = jnp.dot(rows_all, frozen_gate_matrix[0], preferred_element_type=jnp.float32)
    upper = jnp.dot(rows_all, frozen_up_matrix[0], preferred_element_type=jnp.float32)
    hidden = (jax.nn.silu(gate) * upper).astype(jnp.bfloat16)
    low = jnp.einsum("nf,rf->nr", hidden, in_b, preferred_element_type=jnp.float32).astype(
        jnp.bfloat16
    )
    low_back = lax.all_to_all(low.reshape(devices, tok_dev, rank), "exp", 0, 0, tiled=True)
    result = jnp.dot(
        hidden, frozen_down_matrix[0], preferred_element_type=jnp.float32
    ) + adapter_scale * jnp.dot(low, out_b, preferred_element_type=jnp.float32)
    result = (expert_weight[:, None] * result).astype(jnp.bfloat16)
    combined = lax.psum_scatter(result, "exp", scatter_dimension=0, tiled=True)[None]

    grad_in = adapter_scale * jnp.einsum(
        "nr,nf->rf", back, hidden, preferred_element_type=jnp.float32
    )
    weighted = (low_back.astype(jnp.float32) * own_table[:, :, None]).astype(jnp.bfloat16)
    grad_out = adapter_scale * jnp.einsum(
        "etr,td->erd", weighted, own_grads, preferred_element_type=jnp.float32
    )
    grad_out = lax.psum_scatter(
        grad_out.reshape(devices * rank, width), "exp", scatter_dimension=0, tiled=True
    )

    levels = lax.axis_size("rep").bit_length() - 1
    joined_rows = jnp.concatenate((adapter_input_factor[0], adapter_output_factor[0]), axis=2)
    branches = [partial(swap_with, level_bit=level_value) for level_value in range(levels)]
    gossip_neighbor = lax.switch(training_step_index[0] % levels, branches, joined_rows)
    units = adapter_input_factor.shape[3]
    mean_in = 0.5 * (adapter_input_factor[0] + gossip_neighbor[:, :, :units])
    mean_out = 0.5 * (adapter_output_factor[0] + gossip_neighbor[:, :, units:])
    power = (training_step_index[0] + 1).astype(jnp.float32)
    fix_one = 1.0 - jnp.power(jnp.float32(beta_one), power)
    fix_two = 1.0 - jnp.power(jnp.float32(beta_two), power)
    new_in, new_first_in, new_second_in = adam_update(
        mean_in, grad_in[None], input_first_moment[0], input_second_moment[0], fix_one, fix_two
    )
    new_out, new_first_out, new_second_out = adam_update(
        mean_out, grad_out[None], output_first_moment[0], output_second_moment[0], fix_one, fix_two
    )
    return (
        combined,
        new_in[None],
        new_out[None],
        new_first_in[None],
        new_first_out[None],
        new_second_in[None],
        new_second_out[None],
    )


def solution(mesh):
    placed = (
        P("rep", "exp", None),
        P("rep", "exp", None),
        P("rep", "exp", None),
        P("rep", "exp", None),
        P(),
        P(),
        P("exp", None, None),
        P("exp", None, None),
        P("exp", None, None),
        P("rep", "exp", None, None),
        P("rep", "exp", None, None),
        P("rep", "exp", None, None),
        P("rep", "exp", None, None),
        P("rep", "exp", None, None),
        P("rep", "exp", None, None),
    )
    return jax.shard_map(
        per_device,
        mesh=mesh,
        in_specs=placed,
        out_specs=(
            P("rep", "exp", None),
            P("rep", "exp", None, None),
            P("rep", "exp", None, None),
            P("rep", "exp", None, None),
            P("rep", "exp", None, None),
            P("rep", "exp", None, None),
            P("rep", "exp", None, None),
        ),
        check_vma=False,
    )
```

```python
from functools import partial

import jax
import jax.numpy as jnp
from jax import lax
from jax.experimental import pallas as pl
from jax.experimental.pallas import tpu as pltpu
from jax.sharding import PartitionSpec as P

adapter_scale = 0.5
beta_one = 0.9
beta_two = 0.999
learn_rate = 0.02
weight_decay = 0.01
epsilon = 1e-08
MESH = pl.DeviceIdType.MESH


def as_sent(x):
    return jax.tree.map(lambda a: a.astype(jnp.bfloat16) if a.dtype == jnp.float32 else a, x)


def partner(value, axis, stride):
    mask = 2**stride
    pairs = [(source, source ^ mask) for source in range(lax.axis_size(axis))]
    return lax.ppermute(value, axis, pairs)


def swap_with(joined_rows, level_bit):
    return jax.tree.map(
        lambda part, own: part.astype(own.dtype),
        partner(as_sent(joined_rows), "rep", level_bit),
        joined_rows,
    )


def adam_update(averaged, gradient, first_moment, second_moment, fix_one, fix_two):
    new_first = beta_one * first_moment + (1.0 - beta_one) * gradient
    new_second = beta_two * second_moment + (1.0 - beta_two) * gradient * gradient
    stepped = new_first / fix_one / (jnp.sqrt(new_second / fix_two) + epsilon)
    return (averaged - learn_rate * (stepped + weight_decay * averaged), new_first, new_second)


def layer_kernel(
    x_ref,
    cot_ref,
    table_ref,
    cap_ref,
    gate_ref,
    up_ref,
    down_ref,
    in_ref,
    out_ref,
    comb_ref,
    gin_ref,
    gout_ref,
    rows,
    part,
    from_core,
    from_y,
    from_low,
    from_high,
    hid,
    tables,
    low_mine,
    low_got,
    back_mine,
    back_got,
    grad_mine,
    grad_got,
    rows_s,
    rows_r,
    core_s,
    core_r,
    y_s,
    y_r,
    z_s,
    zu_r,
    zd_r,
    tab_s,
    tab_r,
    low_s,
    low_r,
    back_s,
    back_r,
    grad_s,
    grad_r,
):
    n = 16
    depth = 4
    f32 = jnp.float32
    bf16 = jnp.bfloat16
    me = lax.axis_index("exp")
    z, y, c = me // 4, (me // 2) % 2, me % 2
    tok = cot_ref.shape[0]
    rank = in_ref.shape[0]
    core_mate = me + 1 - 2 * c
    y_mate = me + 2 - 4 * y

    def copy(src, dst, send, recv, device):
        return pltpu.make_async_remote_copy(
            src_ref=src,
            dst_ref=dst,
            send_sem=send,
            recv_sem=recv,
            device_id={"exp": device},
            device_id_type=MESH,
        )

    def order(s):
        table = ((0, 1, 2, 3), (1, 2, 0, 3), (2, 1, 3, 0), (3, 2, 1, 0))
        value = s * 0
        for row in range(depth):
            for col in range(depth):
                value = jnp.where((z == row) & (s == col), table[row][col], value)
        return value

    def send_rows(kind, slot, device):
        return copy(rows.at[slot], rows.at[slot], rows_s.at[kind, slot], rows_r.at[slot], device)

    def send_table(d):
        return copy(
            table_ref, tables.at[me], tab_s.at[d], tab_r.at[me], lax.rem(me + d, n)
        )

    def send_low(t):
        return copy(low_mine.at[t], low_got.at[me], low_s.at[t], low_r.at[me], t)

    def send_back(t):
        return copy(back_mine.at[t], back_got.at[me], back_s.at[t], back_r.at[me], t)

    def send_grad(t):
        return copy(grad_mine.at[t], grad_got.at[me], grad_s.at[t], grad_r.at[me], t)

    def send_core(zt, yt):
        return copy(
            part.at[zt * 4 + yt * 2 + 1 - c],
            from_core.at[zt * 2 + yt],
            core_s.at[zt * 2 + yt],
            core_r.at[zt * 2 + yt],
            core_mate,
        )

    def send_y(zt):
        return copy(
            part.at[zt * 4 + (1 - y) * 2 + c], from_y.at[zt], y_s.at[zt], y_r.at[zt], y_mate
        )

    def send_up(zt):
        return copy(
            part.at[zt * 4 + y * 2 + c], from_low.at[zt], z_s.at[zt], zu_r.at[zt], me + 4
        )

    def send_down(zt):
        return copy(
            part.at[zt * 4 + y * 2 + c], from_high.at[zt], z_s.at[zt], zd_r.at[zt], me - 4
        )

    rows[me] = x_ref[...]
    tables[me] = table_ref[...]
    barrier = pltpu.get_barrier_semaphore()

    @pl.loop(1, n)
    def _(d):
        pl.semaphore_signal(
            barrier, inc=1, device_id={"exp": lax.rem(me + d, n)}, device_id_type=MESH
        )

    pl.semaphore_wait(barrier, n - 1)

    @pl.loop(1, n)
    def _(d):
        send_table(d).start()

    def forward(zz, act):
        slot = zz * 4 + y * 2 + c

        @pl.when((zz <= z) & (z < depth - 1))
        def _():
            act(send_rows(0, slot, me + 4))

        @pl.when((zz >= z) & (z > 0))
        def _():
            act(send_rows(1, slot, me - 4))

        act(send_rows(2, slot, y_mate))
        act(send_rows(3, slot, core_mate))

    forward(z, lambda one: one.start())

    @pl.loop(1, n)
    def _(d):
        source = lax.rem(me + d, n)
        copy(table_ref, tables.at[source], tab_s.at[d], tab_r.at[source], source).wait_recv()

    later = lax.broadcasted_iota(jnp.int32, (tok, tok), 1)
    sooner = lax.broadcasted_iota(jnp.int32, (tok, tok), 0)
    strictly = (sooner < later).astype(bf16)
    before = jnp.zeros((n, 1), f32)
    for source in range(n):
        weight = tables[source]
        hit = (weight > 0).astype(f32)
        within = jnp.dot(hit.astype(bf16), strictly, preferred_element_type=f32)
        kept = before + within < cap_ref[...]
        tables[source] = jnp.where(kept, weight, 0.0)
        before = before + jnp.sum(hit, axis=1, keepdims=True)

    own_table = tables.at[me]
    lane = lax.broadcasted_iota(jnp.int32, (tok, n), 1)

    def transposed_dot(a, b):
        return lax.dot_general(a, b, (((1,), (1,)), ((), ())), preferred_element_type=f32)

    def expert_pair(zt, yt):
        first = zt * 4 + yt * 2
        x = jnp.concatenate((rows[first, 0:tok, :], rows[first + 1, 0:tok, :]), axis=0)
        gate = jnp.dot(x, gate_ref[...], preferred_element_type=f32)
        upper = jnp.dot(x, up_ref[...], preferred_element_type=f32)
        hidden = (gate / (1.0 + jnp.exp(-gate)) * upper).astype(bf16)
        hid[first] = hidden[:tok]
        hid[first + 1] = hidden[tok:]
        low_t = transposed_dot(in_ref[...], hidden).astype(bf16)
        low = transposed_dot(hidden, in_ref[...]).astype(bf16)
        result = jnp.dot(hidden, down_ref[...], preferred_element_type=f32)
        result = result + adapter_scale * jnp.dot(low, out_ref[...], preferred_element_type=f32)
        for k in range(2):
            t = first + k
            scale = jnp.sum(
                jnp.where(lane == me, tables[t].T, 0.0), axis=1, keepdims=True
            )
            part[t] = (scale * result[k * tok : (k + 1) * tok]).astype(bf16)
            back = transposed_dot(rows[t, tok : tok + rank, :], cot_ref[...])
            back = (back * own_table[pl.ds(t, 1), :]).astype(bf16)
            low_k = low_t[:, k * tok : (k + 1) * tok]

            @pl.when(t == me)
            def _():
                low_got[t] = low_k
                back_got[t] = back

            @pl.when(t != me)
            def _():
                low_mine[t] = low_k
                back_mine[t] = back
                send_low(t).start()
                send_back(t).start()

        send_core(zt, yt).start()

    def wait_rows(slot):
        send_rows(3, slot, core_mate).wait_recv()

    def add_core(zt, yt):
        send_core(zt, yt).wait_recv()
        t = zt * 4 + yt * 2 + c
        part[t] = (part[t].astype(f32) + from_core[zt * 2 + yt].astype(f32)).astype(bf16)

    @pl.loop(0, depth + 2)
    def _(s):
        now = order(s)
        last = order(s - 1)
        older = order(s - 2)

        @pl.when((s > 0) & (s < depth))
        def _():
            wait_rows(now * 4 + y * 2 + c)
            forward(now, lambda one: one.start())

        @pl.when((s > 0) & (s <= depth))
        def _():
            slot = last * 4 + (1 - y) * 2 + c
            wait_rows(slot)
            send_rows(3, slot, core_mate).start()

        @pl.loop(0, 2)
        def _(which):
            zt = jnp.where(which == 0, now, last)
            yt = jnp.where(which == 0, y, 1 - y)

            @pl.when((s >= which) & (s < depth + which))
            def _():
                wait_rows(zt * 4 + yt * 2 + 1 - c)
                expert_pair(zt, yt)

        @pl.when(s >= 2)
        def _():
            t = older * 4 + y * 2 + c
            send_y(older).wait_recv()
            part[t] = (part[t].astype(f32) + from_y[older].astype(f32)).astype(bf16)

            @pl.when((z == 0) & (older > 0))
            def _():
                send_up(older).start()

            @pl.when((z == depth - 1) & (older < depth - 1))
            def _():
                send_down(older).start()

        @pl.when((s > 0) & (s <= depth))
        def _():
            add_core(last, 1 - y)
            send_y(last).start()

        @pl.when(s < depth)
        def _():
            add_core(now, y)

    @pl.when((z > 0) & (z < depth - 1))
    def _():
        @pl.loop(0, depth - 1)
        def _(item):
            up_first = jnp.where(item == 0, 2, jnp.where(item == 1, 3, 0))
            zt = jnp.where(z == 1, up_first, 3 - up_first)
            t = zt * 4 + y * 2 + c

            @pl.when(zt > z)
            def _():
                send_up(zt).wait_recv()
                part[t] = (part[t].astype(f32) + from_low[zt].astype(f32)).astype(bf16)
                send_up(zt).start()

            @pl.when(zt < z)
            def _():
                send_down(zt).wait_recv()
                part[t] = (part[t].astype(f32) + from_high[zt].astype(f32)).astype(bf16)
                send_down(zt).start()

    @pl.loop(0, n)
    def _(t):
        @pl.when(t != me)
        def _():
            copy(low_mine.at[t], low_got.at[t], low_s.at[t], low_r.at[t], t).wait_recv()

        weighted = (low_got[t].astype(f32) * own_table[pl.ds(t, 1), :]).astype(bf16)
        grad = adapter_scale * jnp.dot(weighted, cot_ref[...], preferred_element_type=f32)

        @pl.when(t == me)
        def _():
            grad_got[t] = grad.astype(bf16)

        @pl.when(t != me)
        def _():
            grad_mine[t] = grad.astype(bf16)
            send_grad(t).start()

    gin_ref[...] = jnp.zeros_like(gin_ref)

    @pl.loop(0, n)
    def _(t):
        @pl.when(t != me)
        def _():
            copy(back_mine.at[t], back_got.at[t], back_s.at[t], back_r.at[t], t).wait_recv()

        gin_ref[...] += adapter_scale * jnp.dot(
            back_got[t], hid[t], preferred_element_type=f32
        )

    gout_ref[...] = jnp.zeros_like(gout_ref)

    @pl.loop(0, n)
    def _(t):
        @pl.when(t != me)
        def _():
            copy(grad_mine.at[t], grad_got.at[t], grad_s.at[t], grad_r.at[t], t).wait_recv()

        gout_ref[...] += grad_got[t].astype(f32)

    @pl.when(z > 0)
    def _():
        send_up(z).wait_recv()

    @pl.when(z < depth - 1)
    def _():
        send_down(z).wait_recv()

    @pl.when(z == 0)
    def _():
        comb_ref[...] = (part[me].astype(f32) + from_high[z].astype(f32)).astype(bf16)

    @pl.when(z == depth - 1)
    def _():
        comb_ref[...] = (part[me].astype(f32) + from_low[z].astype(f32)).astype(bf16)

    @pl.when((z > 0) & (z < depth - 1))
    def _():
        comb_ref[...] = (
            part[me].astype(f32) + from_low[z].astype(f32) + from_high[z].astype(f32)
        ).astype(bf16)

    @pl.loop(0, depth)
    def _(zt):
        forward(zt, lambda one: one.wait_send())
        send_rows(3, zt * 4 + (1 - y) * 2 + c, core_mate).wait_send()
        send_core(zt, 0).wait_send()
        send_core(zt, 1).wait_send()
        send_y(zt).wait_send()

        @pl.when(zt != z)
        def _():
            copy(part.at[zt], from_low.at[zt], z_s.at[zt], zu_r.at[zt], y_mate).wait_send()

    @pl.loop(1, n)
    def _(d):
        t = lax.rem(me + d, n)
        send_table(d).wait_send()
        send_low(t).wait_send()
        send_back(t).wait_send()
        send_grad(t).wait_send()


def layer(x, cot, table, cap, gate, up, down, in_b, out_b):
    n = table.shape[0]
    tok, width = cot.shape
    rank, units = in_b.shape
    vmem = pl.BlockSpec(memory_space=pltpu.VMEM)
    bf16 = jnp.bfloat16
    dma = pltpu.SemaphoreType.DMA
    return pl.pallas_call(
        layer_kernel,
        out_shape=(
            jax.ShapeDtypeStruct((tok, width), bf16),
            jax.ShapeDtypeStruct((rank, units), jnp.float32),
            jax.ShapeDtypeStruct((rank, width), jnp.float32),
        ),
        in_specs=[vmem] * 9,
        out_specs=(vmem, vmem, vmem),
        scratch_shapes=[
            pltpu.VMEM((n, tok + rank, width), bf16),
            pltpu.VMEM((n, tok, width), bf16),
            pltpu.VMEM((n // 2, tok, width), bf16),
            pltpu.VMEM((n // 4, tok, width), bf16),
            pltpu.VMEM((n // 4, tok, width), bf16),
            pltpu.VMEM((n // 4, tok, width), bf16),
            pltpu.VMEM((n, tok, units), bf16),
            pltpu.VMEM((n, n, tok), jnp.float32),
            pltpu.VMEM((n, rank, tok), bf16),
            pltpu.VMEM((n, rank, tok), bf16),
            pltpu.VMEM((n, rank, tok), bf16),
            pltpu.VMEM((n, rank, tok), bf16),
            pltpu.VMEM((n, rank, width), bf16),
            pltpu.VMEM((n, rank, width), bf16),
            dma((4, n)),
            dma((n,)),
            dma((n // 2,)),
            dma((n // 2,)),
            dma((n // 4,)),
            dma((n // 4,)),
            dma((n // 4,)),
            dma((n // 4,)),
            dma((n // 4,)),
        ]
        + [dma((n,))] * 8,
        compiler_params=pltpu.CompilerParams(
            collective_id=0, has_side_effects=True, vmem_limit_bytes=60 * 1024 * 1024
        ),
        cost_estimate=pl.CostEstimate(
            flops=20_000_000_000, bytes_accessed=30_000_000, transcendentals=0
        ),
    )(x, cot, table, cap, gate, up, down, in_b, out_b)


def per_device(
    tokens,
    cotangent,
    routes,
    router_pair_weight,
    capacity,
    training_step_index,
    frozen_gate_matrix,
    frozen_up_matrix,
    frozen_down_matrix,
    adapter_input_factor,
    adapter_output_factor,
    input_first_moment,
    output_first_moment,
    input_second_moment,
    output_second_moment,
):
    devices = lax.axis_size("exp")
    assert frozen_gate_matrix.shape[0] == 1 and devices == 16
    own_grads = cotangent[0]
    in_b = adapter_input_factor[0, 0].astype(jnp.bfloat16)
    out_b = adapter_output_factor[0, 0].astype(jnp.bfloat16)

    hits = routes[0][None, :, :] == jnp.arange(devices, dtype=jnp.int32)[:, None, None]
    table = jnp.sum(
        jnp.where(hits, router_pair_weight[0].astype(jnp.float32)[None], 0.0), axis=2
    )
    combined, grad_in, grad_out = layer(
        jnp.concatenate((tokens[0], out_b), axis=0),
        own_grads,
        table,
        capacity.astype(jnp.float32)[:, None],
        frozen_gate_matrix[0],
        frozen_up_matrix[0],
        frozen_down_matrix[0],
        in_b,
        out_b,
    )
    combined = combined[None]

    levels = lax.axis_size("rep").bit_length() - 1
    joined_rows = jnp.concatenate((adapter_input_factor[0], adapter_output_factor[0]), axis=2)
    branches = [partial(swap_with, level_bit=level_value) for level_value in range(levels)]
    gossip_neighbor = lax.switch(training_step_index[0] % levels, branches, joined_rows)
    units = adapter_input_factor.shape[3]
    mean_in = 0.5 * (adapter_input_factor[0] + gossip_neighbor[:, :, :units])
    mean_out = 0.5 * (adapter_output_factor[0] + gossip_neighbor[:, :, units:])
    power = (training_step_index[0] + 1).astype(jnp.float32)
    fix_one = 1.0 - jnp.power(jnp.float32(beta_one), power)
    fix_two = 1.0 - jnp.power(jnp.float32(beta_two), power)
    new_in, new_first_in, new_second_in = adam_update(
        mean_in, grad_in[None], input_first_moment[0], input_second_moment[0], fix_one, fix_two
    )
    new_out, new_first_out, new_second_out = adam_update(
        mean_out, grad_out[None], output_first_moment[0], output_second_moment[0], fix_one, fix_two
    )
    return (
        combined,
        new_in[None],
        new_out[None],
        new_first_in[None],
        new_first_out[None],
        new_second_in[None],
        new_second_out[None],
    )


def solution(mesh):
    placed = (
        P("rep", "exp", None),
        P("rep", "exp", None),
        P("rep", "exp", None),
        P("rep", "exp", None),
        P(),
        P(),
        P("exp", None, None),
        P("exp", None, None),
        P("exp", None, None),
        P("rep", "exp", None, None),
        P("rep", "exp", None, None),
        P("rep", "exp", None, None),
        P("rep", "exp", None, None),
        P("rep", "exp", None, None),
        P("rep", "exp", None, None),
    )
    return jax.shard_map(
        per_device,
        mesh=mesh,
        in_specs=placed,
        out_specs=(
            P("rep", "exp", None),
            P("rep", "exp", None, None),
            P("rep", "exp", None, None),
            P("rep", "exp", None, None),
            P("rep", "exp", None, None),
            P("rep", "exp", None, None),
            P("rep", "exp", None, None),
        ),
        check_vma=False,
    )
```

```python
from functools import partial

import jax
import jax.numpy as jnp
from jax import lax
from jax.experimental import pallas as pl
from jax.experimental.pallas import tpu as pltpu
from jax.sharding import PartitionSpec as P

adapter_scale = 0.5
beta_one = 0.9
beta_two = 0.999
learn_rate = 0.02
weight_decay = 0.01
epsilon = 1e-08
MESH = pl.DeviceIdType.MESH


def as_sent(x):
    return jax.tree.map(lambda a: a.astype(jnp.bfloat16) if a.dtype == jnp.float32 else a, x)


def partner(value, axis, stride):
    mask = 2**stride
    pairs = [(source, source ^ mask) for source in range(lax.axis_size(axis))]
    return lax.ppermute(value, axis, pairs)


def swap_with(joined_rows, level_bit):
    return jax.tree.map(
        lambda part, own: part.astype(own.dtype),
        partner(as_sent(joined_rows), "rep", level_bit),
        joined_rows,
    )


def adam_update(averaged, gradient, first_moment, second_moment, fix_one, fix_two):
    new_first = beta_one * first_moment + (1.0 - beta_one) * gradient
    new_second = beta_two * second_moment + (1.0 - beta_two) * gradient * gradient
    stepped = new_first / fix_one / (jnp.sqrt(new_second / fix_two) + epsilon)
    return (averaged - learn_rate * (stepped + weight_decay * averaged), new_first, new_second)


def layer_kernel(
    x_ref,
    cot_ref,
    table_ref,
    cap_ref,
    gate_ref,
    up_ref,
    down_ref,
    in_ref,
    out_ref,
    comb_ref,
    gin_ref,
    gout_ref,
    rows,
    part,
    from_core,
    from_y,
    from_low,
    from_high,
    hid,
    tables,
    low_mine,
    low_got,
    back_mine,
    back_got,
    grad_mine,
    grad_got,
    rows_s,
    rows_r,
    core_s,
    core_r,
    y_s,
    y_r,
    z_s,
    zu_r,
    zd_r,
    tab_s,
    tab_r,
    low_s,
    low_r,
    back_s,
    back_r,
    grad_s,
    grad_r,
):
    n = 16
    depth = 4
    f32 = jnp.float32
    bf16 = jnp.bfloat16
    me = lax.axis_index("exp")
    z, y, c = me // 4, (me // 2) % 2, me % 2
    tok = cot_ref.shape[0]
    rank = in_ref.shape[0]
    core_mate = me + 1 - 2 * c
    y_mate = me + 2 - 4 * y

    def copy(src, dst, send, recv, device):
        return pltpu.make_async_remote_copy(
            src_ref=src,
            dst_ref=dst,
            send_sem=send,
            recv_sem=recv,
            device_id={"exp": device},
            device_id_type=MESH,
        )

    def order(s):
        table = ((0, 1, 2, 3), (1, 2, 0, 3), (2, 1, 3, 0), (3, 2, 1, 0))
        value = s * 0
        for row in range(depth):
            for col in range(depth):
                value = jnp.where((z == row) & (s == col), table[row][col], value)
        return value

    def send_rows(kind, slot, device):
        return copy(rows.at[slot], rows.at[slot], rows_s.at[kind, slot], rows_r.at[slot], device)

    def send_table(d):
        return copy(
            table_ref, tables.at[me], tab_s.at[d], tab_r.at[me], lax.rem(me + d, n)
        )

    def send_low(t):
        return copy(low_mine.at[t], low_got.at[me], low_s.at[t], low_r.at[me], t)

    def send_back(t):
        return copy(back_mine.at[t], back_got.at[me], back_s.at[t], back_r.at[me], t)

    def send_grad(t):
        return copy(grad_mine.at[t], grad_got.at[me], grad_s.at[t], grad_r.at[me], t)

    def send_core(zt, yt):
        return copy(
            part.at[zt * 4 + yt * 2 + 1 - c],
            from_core.at[zt * 2 + yt],
            core_s.at[zt * 2 + yt],
            core_r.at[zt * 2 + yt],
            core_mate,
        )

    def send_y(zt):
        return copy(
            part.at[zt * 4 + (1 - y) * 2 + c], from_y.at[zt], y_s.at[zt], y_r.at[zt], y_mate
        )

    def send_up(zt):
        return copy(
            part.at[zt * 4 + y * 2 + c], from_low.at[zt], z_s.at[zt], zu_r.at[zt], me + 4
        )

    def send_down(zt):
        return copy(
            part.at[zt * 4 + y * 2 + c], from_high.at[zt], z_s.at[zt], zd_r.at[zt], me - 4
        )

    rows[me, 0:tok, :] = x_ref[...]
    rows[me, tok : tok + rank, :] = out_ref[...]
    tables[me] = table_ref[...]
    barrier = pltpu.get_barrier_semaphore()

    @pl.loop(1, n)
    def _(d):
        pl.semaphore_signal(
            barrier, inc=1, device_id={"exp": lax.rem(me + d, n)}, device_id_type=MESH
        )

    pl.semaphore_wait(barrier, n - 1)

    @pl.loop(1, n)
    def _(d):
        send_table(d).start()

    def forward(zz, act):
        slot = zz * 4 + y * 2 + c

        @pl.when((zz <= z) & (z < depth - 1))
        def _():
            act(send_rows(0, slot, me + 4))

        @pl.when((zz >= z) & (z > 0))
        def _():
            act(send_rows(1, slot, me - 4))

        act(send_rows(2, slot, y_mate))
        act(send_rows(3, slot, core_mate))

    forward(z, lambda one: one.start())

    @pl.loop(1, n)
    def _(d):
        source = lax.rem(me + d, n)
        copy(table_ref, tables.at[source], tab_s.at[d], tab_r.at[source], source).wait_recv()

    later = lax.broadcasted_iota(jnp.int32, (tok, tok), 1)
    sooner = lax.broadcasted_iota(jnp.int32, (tok, tok), 0)
    strictly = (sooner < later).astype(bf16)
    before = jnp.zeros((n, 1), f32)
    for source in range(n):
        weight = tables[source]
        hit = (weight > 0).astype(f32)
        within = jnp.dot(hit.astype(bf16), strictly, preferred_element_type=f32)
        kept = before + within < cap_ref[...]
        tables[source] = jnp.where(kept, weight, 0.0)
        before = before + jnp.sum(hit, axis=1, keepdims=True)

    own_table = tables.at[me]
    lane = lax.broadcasted_iota(jnp.int32, (tok, n), 1)

    def transposed_dot(a, b):
        return lax.dot_general(a, b, (((1,), (1,)), ((), ())), preferred_element_type=f32)

    def expert_pair(zt, yt):
        first = zt * 4 + yt * 2
        x = jnp.concatenate((rows[first, 0:tok, :], rows[first + 1, 0:tok, :]), axis=0)
        gate = jnp.dot(x, gate_ref[...], preferred_element_type=f32)
        upper = jnp.dot(x, up_ref[...], preferred_element_type=f32)
        hidden = (gate / (1.0 + jnp.exp(-gate)) * upper).astype(bf16)
        hid[first] = hidden[:tok]
        hid[first + 1] = hidden[tok:]
        low_t = transposed_dot(in_ref[...], hidden).astype(bf16)
        low = transposed_dot(hidden, in_ref[...]).astype(bf16)
        result = jnp.dot(hidden, down_ref[...], preferred_element_type=f32)
        result = result + adapter_scale * jnp.dot(low, out_ref[...], preferred_element_type=f32)
        for k in range(2):
            t = first + k
            scale = jnp.sum(
                jnp.where(lane == me, tables[t].T, 0.0), axis=1, keepdims=True
            )
            part[t] = (scale * result[k * tok : (k + 1) * tok]).astype(bf16)
            back = transposed_dot(rows[t, tok : tok + rank, :], cot_ref[...])
            back = (back * own_table[pl.ds(t, 1), :]).astype(bf16)
            low_k = low_t[:, k * tok : (k + 1) * tok]

            @pl.when(t == me)
            def _():
                low_got[t] = low_k
                back_got[t] = back

            @pl.when(t != me)
            def _():
                low_mine[t] = low_k
                back_mine[t] = back
                send_low(t).start()
                send_back(t).start()

        send_core(zt, yt).start()

    def wait_rows(slot):
        send_rows(3, slot, core_mate).wait_recv()

    def add_core(zt, yt):
        send_core(zt, yt).wait_recv()
        t = zt * 4 + yt * 2 + c
        part[t] = (part[t].astype(f32) + from_core[zt * 2 + yt].astype(f32)).astype(bf16)

    @pl.loop(0, depth + 2)
    def _(s):
        now = order(s)
        last = order(s - 1)
        older = order(s - 2)

        @pl.when((s > 0) & (s < depth))
        def _():
            wait_rows(now * 4 + y * 2 + c)
            forward(now, lambda one: one.start())

        @pl.when((s > 0) & (s <= depth))
        def _():
            slot = last * 4 + (1 - y) * 2 + c
            wait_rows(slot)
            send_rows(3, slot, core_mate).start()

        @pl.loop(0, 2)
        def _(which):
            zt = jnp.where(which == 0, now, last)
            yt = jnp.where(which == 0, y, 1 - y)

            @pl.when((s >= which) & (s < depth + which))
            def _():
                wait_rows(zt * 4 + yt * 2 + 1 - c)
                expert_pair(zt, yt)

        @pl.when(s >= 2)
        def _():
            t = older * 4 + y * 2 + c
            send_y(older).wait_recv()
            part[t] = (part[t].astype(f32) + from_y[older].astype(f32)).astype(bf16)

            @pl.when((z == 0) & (older > 0))
            def _():
                send_up(older).start()

            @pl.when((z == depth - 1) & (older < depth - 1))
            def _():
                send_down(older).start()

        @pl.when((s > 0) & (s <= depth))
        def _():
            add_core(last, 1 - y)
            send_y(last).start()

        @pl.when(s < depth)
        def _():
            add_core(now, y)

    @pl.loop(0, n)
    def _(t):
        @pl.when(t != me)
        def _():
            copy(low_mine.at[t], low_got.at[t], low_s.at[t], low_r.at[t], t).wait_recv()

        weighted = (low_got[t].astype(f32) * own_table[pl.ds(t, 1), :]).astype(bf16)
        grad = adapter_scale * jnp.dot(weighted, cot_ref[...], preferred_element_type=f32)

        @pl.when(t == me)
        def _():
            grad_got[t] = grad.astype(bf16)

        @pl.when(t != me)
        def _():
            grad_mine[t] = grad.astype(bf16)
            send_grad(t).start()

    @pl.when((z > 0) & (z < depth - 1))
    def _():
        @pl.loop(0, depth - 1)
        def _(item):
            up_first = jnp.where(item == 0, 2, jnp.where(item == 1, 3, 0))
            zt = jnp.where(z == 1, up_first, 3 - up_first)
            t = zt * 4 + y * 2 + c

            @pl.when(zt > z)
            def _():
                send_up(zt).wait_recv()
                part[t] = (part[t].astype(f32) + from_low[zt].astype(f32)).astype(bf16)
                send_up(zt).start()

            @pl.when(zt < z)
            def _():
                send_down(zt).wait_recv()
                part[t] = (part[t].astype(f32) + from_high[zt].astype(f32)).astype(bf16)
                send_down(zt).start()

    gin_ref[...] = jnp.zeros_like(gin_ref)

    @pl.loop(0, n)
    def _(t):
        @pl.when(t != me)
        def _():
            copy(back_mine.at[t], back_got.at[t], back_s.at[t], back_r.at[t], t).wait_recv()

        gin_ref[...] += adapter_scale * jnp.dot(
            back_got[t], hid[t], preferred_element_type=f32
        )

    gout_ref[...] = jnp.zeros_like(gout_ref)

    @pl.loop(0, n)
    def _(t):
        @pl.when(t != me)
        def _():
            copy(grad_mine.at[t], grad_got.at[t], grad_s.at[t], grad_r.at[t], t).wait_recv()

        gout_ref[...] += grad_got[t].astype(f32)

    @pl.when(z > 0)
    def _():
        send_up(z).wait_recv()

    @pl.when(z < depth - 1)
    def _():
        send_down(z).wait_recv()

    @pl.when(z == 0)
    def _():
        comb_ref[...] = (part[me].astype(f32) + from_high[z].astype(f32)).astype(bf16)

    @pl.when(z == depth - 1)
    def _():
        comb_ref[...] = (part[me].astype(f32) + from_low[z].astype(f32)).astype(bf16)

    @pl.when((z > 0) & (z < depth - 1))
    def _():
        comb_ref[...] = (
            part[me].astype(f32) + from_low[z].astype(f32) + from_high[z].astype(f32)
        ).astype(bf16)

    @pl.loop(0, depth)
    def _(zt):
        forward(zt, lambda one: one.wait_send())
        send_rows(3, zt * 4 + (1 - y) * 2 + c, core_mate).wait_send()
        send_core(zt, 0).wait_send()
        send_core(zt, 1).wait_send()
        send_y(zt).wait_send()

        @pl.when(zt != z)
        def _():
            copy(part.at[zt], from_low.at[zt], z_s.at[zt], zu_r.at[zt], y_mate).wait_send()

    @pl.loop(1, n)
    def _(d):
        t = lax.rem(me + d, n)
        send_table(d).wait_send()
        send_low(t).wait_send()
        send_back(t).wait_send()
        send_grad(t).wait_send()


def layer(x, cot, table, cap, gate, up, down, in_b, out_b):
    n = table.shape[0]
    tok, width = cot.shape
    rank, units = in_b.shape
    vmem = pl.BlockSpec(memory_space=pltpu.VMEM)
    bf16 = jnp.bfloat16
    dma = pltpu.SemaphoreType.DMA
    return pl.pallas_call(
        layer_kernel,
        out_shape=(
            jax.ShapeDtypeStruct((tok, width), bf16),
            jax.ShapeDtypeStruct((rank, units), jnp.float32),
            jax.ShapeDtypeStruct((rank, width), jnp.float32),
        ),
        in_specs=[vmem] * 9,
        out_specs=(vmem, vmem, vmem),
        scratch_shapes=[
            pltpu.VMEM((n, tok + rank, width), bf16),
            pltpu.VMEM((n, tok, width), bf16),
            pltpu.VMEM((n // 2, tok, width), bf16),
            pltpu.VMEM((n // 4, tok, width), bf16),
            pltpu.VMEM((n // 4, tok, width), bf16),
            pltpu.VMEM((n // 4, tok, width), bf16),
            pltpu.VMEM((n, tok, units), bf16),
            pltpu.VMEM((n, n, tok), jnp.float32),
            pltpu.VMEM((n, rank, tok), bf16),
            pltpu.VMEM((n, rank, tok), bf16),
            pltpu.VMEM((n, rank, tok), bf16),
            pltpu.VMEM((n, rank, tok), bf16),
            pltpu.VMEM((n, rank, width), bf16),
            pltpu.VMEM((n, rank, width), bf16),
            dma((4, n)),
            dma((n,)),
            dma((n // 2,)),
            dma((n // 2,)),
            dma((n // 4,)),
            dma((n // 4,)),
            dma((n // 4,)),
            dma((n // 4,)),
            dma((n // 4,)),
        ]
        + [dma((n,))] * 8,
        compiler_params=pltpu.CompilerParams(
            collective_id=0, has_side_effects=True, vmem_limit_bytes=60 * 1024 * 1024
        ),
        cost_estimate=pl.CostEstimate(
            flops=20_000_000_000, bytes_accessed=30_000_000, transcendentals=0
        ),
    )(x, cot, table, cap, gate, up, down, in_b, out_b)


def per_device(
    tokens,
    cotangent,
    routes,
    router_pair_weight,
    capacity,
    training_step_index,
    frozen_gate_matrix,
    frozen_up_matrix,
    frozen_down_matrix,
    adapter_input_factor,
    adapter_output_factor,
    input_first_moment,
    output_first_moment,
    input_second_moment,
    output_second_moment,
):
    devices = lax.axis_size("exp")
    assert frozen_gate_matrix.shape[0] == 1 and devices == 16
    own_grads = cotangent[0]
    in_b = adapter_input_factor[0, 0].astype(jnp.bfloat16)
    out_b = adapter_output_factor[0, 0].astype(jnp.bfloat16)

    hits = routes[0][None, :, :] == jnp.arange(devices, dtype=jnp.int32)[:, None, None]
    table = jnp.sum(
        jnp.where(hits, router_pair_weight[0].astype(jnp.float32)[None], 0.0), axis=2
    )
    combined, grad_in, grad_out = layer(
        tokens[0],
        own_grads,
        table,
        capacity.astype(jnp.float32)[:, None],
        frozen_gate_matrix[0],
        frozen_up_matrix[0],
        frozen_down_matrix[0],
        in_b,
        out_b,
    )
    combined = combined[None]

    levels = lax.axis_size("rep").bit_length() - 1
    joined_rows = jnp.concatenate((adapter_input_factor[0], adapter_output_factor[0]), axis=2)
    branches = [partial(swap_with, level_bit=level_value) for level_value in range(levels)]
    gossip_neighbor = lax.switch(training_step_index[0] % levels, branches, joined_rows)
    units = adapter_input_factor.shape[3]
    mean_in = 0.5 * (adapter_input_factor[0] + gossip_neighbor[:, :, :units])
    mean_out = 0.5 * (adapter_output_factor[0] + gossip_neighbor[:, :, units:])
    power = (training_step_index[0] + 1).astype(jnp.float32)
    fix_one = 1.0 - jnp.power(jnp.float32(beta_one), power)
    fix_two = 1.0 - jnp.power(jnp.float32(beta_two), power)
    new_in, new_first_in, new_second_in = adam_update(
        mean_in, grad_in[None], input_first_moment[0], input_second_moment[0], fix_one, fix_two
    )
    new_out, new_first_out, new_second_out = adam_update(
        mean_out, grad_out[None], output_first_moment[0], output_second_moment[0], fix_one, fix_two
    )
    return (
        combined,
        new_in[None],
        new_out[None],
        new_first_in[None],
        new_first_out[None],
        new_second_in[None],
        new_second_out[None],
    )


def solution(mesh):
    placed = (
        P("rep", "exp", None),
        P("rep", "exp", None),
        P("rep", "exp", None),
        P("rep", "exp", None),
        P(),
        P(),
        P("exp", None, None),
        P("exp", None, None),
        P("exp", None, None),
        P("rep", "exp", None, None),
        P("rep", "exp", None, None),
        P("rep", "exp", None, None),
        P("rep", "exp", None, None),
        P("rep", "exp", None, None),
        P("rep", "exp", None, None),
    )
    return jax.shard_map(
        per_device,
        mesh=mesh,
        in_specs=placed,
        out_specs=(
            P("rep", "exp", None),
            P("rep", "exp", None, None),
            P("rep", "exp", None, None),
            P("rep", "exp", None, None),
            P("rep", "exp", None, None),
            P("rep", "exp", None, None),
            P("rep", "exp", None, None),
        ),
        check_vma=False,
    )
```

```python
from functools import partial

import jax
import jax.numpy as jnp
from jax import lax
from jax.experimental import pallas as pl
from jax.experimental.pallas import tpu as pltpu
from jax.sharding import PartitionSpec as P

adapter_scale = 0.5
beta_one = 0.9
beta_two = 0.999
learn_rate = 0.02
weight_decay = 0.01
epsilon = 1e-08
MESH = pl.DeviceIdType.MESH


def as_sent(x):
    return jax.tree.map(lambda a: a.astype(jnp.bfloat16) if a.dtype == jnp.float32 else a, x)


def partner(value, axis, stride):
    mask = 2**stride
    pairs = [(source, source ^ mask) for source in range(lax.axis_size(axis))]
    return lax.ppermute(value, axis, pairs)


def swap_with(joined_rows, level_bit):
    return jax.tree.map(
        lambda part, own: part.astype(own.dtype),
        partner(as_sent(joined_rows), "rep", level_bit),
        joined_rows,
    )


def adam_update(averaged, gradient, first_moment, second_moment, fix_one, fix_two):
    new_first = beta_one * first_moment + (1.0 - beta_one) * gradient
    new_second = beta_two * second_moment + (1.0 - beta_two) * gradient * gradient
    stepped = new_first / fix_one / (jnp.sqrt(new_second / fix_two) + epsilon)
    return (averaged - learn_rate * (stepped + weight_decay * averaged), new_first, new_second)


def layer_kernel(
    x_ref,
    cot_ref,
    table_ref,
    cap_ref,
    gate_ref,
    up_ref,
    down_ref,
    in_ref,
    out_ref,
    comb_ref,
    gin_ref,
    gout_ref,
    rows,
    part,
    from_core,
    from_y,
    from_low,
    from_high,
    hid,
    tables,
    low_mine,
    low_got,
    back_mine,
    back_got,
    grad_mine,
    grad_got,
    rows_s,
    rows_r,
    core_s,
    core_r,
    y_s,
    y_r,
    z_s,
    zu_r,
    zd_r,
    tab_s,
    tab_r,
    low_s,
    low_r,
    back_s,
    back_r,
    grad_s,
    grad_r,
):
    n = 16
    depth = 4
    f32 = jnp.float32
    bf16 = jnp.bfloat16
    me = lax.axis_index("exp")
    z, y, c = me // 4, (me // 2) % 2, me % 2
    tok = cot_ref.shape[0]
    rank = in_ref.shape[0]
    core_mate = me + 1 - 2 * c
    y_mate = me + 2 - 4 * y

    def copy(src, dst, send, recv, device):
        return pltpu.make_async_remote_copy(
            src_ref=src,
            dst_ref=dst,
            send_sem=send,
            recv_sem=recv,
            device_id={"exp": device},
            device_id_type=MESH,
        )

    def order(s):
        table = ((0, 1, 2, 3), (1, 2, 0, 3), (2, 1, 3, 0), (3, 2, 1, 0))
        value = s * 0
        for row in range(depth):
            for col in range(depth):
                value = jnp.where((z == row) & (s == col), table[row][col], value)
        return value

    def send_rows(kind, slot, device):
        return copy(rows.at[slot], rows.at[slot], rows_s.at[kind, slot], rows_r.at[slot], device)

    def send_table(d):
        return copy(
            table_ref, tables.at[me], tab_s.at[d], tab_r.at[me], lax.rem(me + d, n)
        )

    def send_low(t):
        return copy(low_mine.at[t], low_got.at[me], low_s.at[t], low_r.at[me], t)

    def send_back(t):
        return copy(back_mine.at[t], back_got.at[me], back_s.at[t], back_r.at[me], t)

    def send_grad(t):
        return copy(grad_mine.at[t], grad_got.at[me], grad_s.at[t], grad_r.at[me], t)

    def send_core(zt, yt):
        return copy(
            part.at[zt * 4 + yt * 2 + 1 - c],
            from_core.at[zt * 2 + yt],
            core_s.at[zt * 2 + yt],
            core_r.at[zt * 2 + yt],
            core_mate,
        )

    def send_y(zt):
        return copy(
            part.at[zt * 4 + (1 - y) * 2 + c], from_y.at[zt], y_s.at[zt], y_r.at[zt], y_mate
        )

    def send_up(zt):
        return copy(
            part.at[zt * 4 + y * 2 + c], from_low.at[zt], z_s.at[zt], zu_r.at[zt], me + 4
        )

    def send_down(zt):
        return copy(
            part.at[zt * 4 + y * 2 + c], from_high.at[zt], z_s.at[zt], zd_r.at[zt], me - 4
        )

    rows[me, 0:tok, :] = x_ref[...]
    rows[me, tok : tok + rank, :] = out_ref[...]
    tables[me] = table_ref[...]
    barrier = pltpu.get_barrier_semaphore()

    @pl.loop(1, n)
    def _(d):
        pl.semaphore_signal(
            barrier, inc=1, device_id={"exp": lax.rem(me + d, n)}, device_id_type=MESH
        )

    pl.semaphore_wait(barrier, n - 1)

    @pl.loop(1, n)
    def _(d):
        send_table(d).start()

    def forward(zz, act):
        slot = zz * 4 + y * 2 + c

        @pl.when((zz <= z) & (z < depth - 1))
        def _():
            act(send_rows(0, slot, me + 4))

        @pl.when((zz >= z) & (z > 0))
        def _():
            act(send_rows(1, slot, me - 4))

        act(send_rows(2, slot, y_mate))
        act(send_rows(3, slot, core_mate))

    forward(z, lambda one: one.start())

    @pl.loop(1, n)
    def _(d):
        source = lax.rem(me + d, n)
        copy(table_ref, tables.at[source], tab_s.at[d], tab_r.at[source], source).wait_recv()

    later = lax.broadcasted_iota(jnp.int32, (tok, tok), 1)
    sooner = lax.broadcasted_iota(jnp.int32, (tok, tok), 0)
    strictly = (sooner < later).astype(bf16)
    before = jnp.zeros((n, 1), f32)
    for source in range(n):
        weight = tables[source]
        hit = (weight > 0).astype(f32)
        within = jnp.dot(hit.astype(bf16), strictly, preferred_element_type=f32)
        kept = before + within < cap_ref[...]
        tables[source] = jnp.where(kept, weight, 0.0)
        before = before + jnp.sum(hit, axis=1, keepdims=True)

    own_table = tables.at[me]
    lane = lax.broadcasted_iota(jnp.int32, (tok, n), 1)

    def transposed_dot(a, b):
        return lax.dot_general(a, b, (((1,), (1,)), ((), ())), preferred_element_type=f32)

    def expert_pair(zt, yt):
        first = zt * 4 + yt * 2
        x = jnp.concatenate((rows[first, 0:tok, :], rows[first + 1, 0:tok, :]), axis=0)
        gate = jnp.dot(x, gate_ref[...], preferred_element_type=f32)
        upper = jnp.dot(x, up_ref[...], preferred_element_type=f32)
        hidden = (gate / (1.0 + jnp.exp(-gate)) * upper).astype(bf16)
        hid[first] = hidden[:tok]
        hid[first + 1] = hidden[tok:]
        low_t = transposed_dot(in_ref[...], hidden).astype(bf16)
        low = transposed_dot(hidden, in_ref[...]).astype(bf16)
        result = jnp.dot(hidden, down_ref[...], preferred_element_type=f32)
        result = result + adapter_scale * jnp.dot(low, out_ref[...], preferred_element_type=f32)
        for k in range(2):
            t = first + k
            scale = jnp.sum(
                jnp.where(lane == me, tables[t].T, 0.0), axis=1, keepdims=True
            )
            part[t] = (scale * result[k * tok : (k + 1) * tok]).astype(bf16)
            back = transposed_dot(rows[t, tok : tok + rank, :], cot_ref[...])
            back = (back * own_table[pl.ds(t, 1), :]).astype(bf16)
            low_k = low_t[:, k * tok : (k + 1) * tok]

            @pl.when(t == me)
            def _():
                low_got[t] = low_k
                back_got[t] = back

            @pl.when(t != me)
            def _():
                low_mine[t] = low_k
                back_mine[t] = back
                send_low(t).start()
                send_back(t).start()

        send_core(zt, yt).start()

    def wait_rows(slot):
        send_rows(3, slot, core_mate).wait_recv()

    def add_core(zt, yt):
        send_core(zt, yt).wait_recv()
        t = zt * 4 + yt * 2 + c
        part[t] = (part[t].astype(f32) + from_core[zt * 2 + yt].astype(f32)).astype(bf16)

    @pl.loop(0, depth + 2)
    def _(s):
        now = order(s)
        last = order(s - 1)
        older = order(s - 2)

        @pl.when((s > 0) & (s < depth))
        def _():
            wait_rows(now * 4 + y * 2 + c)
            forward(now, lambda one: one.start())

        @pl.when((s > 0) & (s <= depth))
        def _():
            slot = last * 4 + (1 - y) * 2 + c
            wait_rows(slot)
            send_rows(3, slot, core_mate).start()

        @pl.loop(0, 2)
        def _(which):
            zt = jnp.where(which == 0, now, last)
            yt = jnp.where(which == 0, y, 1 - y)

            @pl.when((s >= which) & (s < depth + which))
            def _():
                wait_rows(zt * 4 + yt * 2 + 1 - c)
                expert_pair(zt, yt)

        @pl.when((s > 0) & (s <= depth))
        def _():
            add_core(last, 1 - y)
            send_y(last).start()

        @pl.when(s >= 2)
        def _():
            t = older * 4 + y * 2 + c
            send_y(older).wait_recv()
            part[t] = (part[t].astype(f32) + from_y[older].astype(f32)).astype(bf16)

            @pl.when((z == 0) & (older > 0))
            def _():
                send_up(older).start()

            @pl.when((z == depth - 1) & (older < depth - 1))
            def _():
                send_down(older).start()

        @pl.when(s < depth)
        def _():
            add_core(now, y)

    @pl.when((z > 0) & (z < depth - 1))
    def _():
        @pl.loop(0, depth - 1)
        def _(item):
            up_first = jnp.where(item == 0, 2, jnp.where(item == 1, 3, 0))
            zt = jnp.where(z == 1, up_first, 3 - up_first)
            t = zt * 4 + y * 2 + c

            @pl.when(zt > z)
            def _():
                send_up(zt).wait_recv()
                part[t] = (part[t].astype(f32) + from_low[zt].astype(f32)).astype(bf16)
                send_up(zt).start()

            @pl.when(zt < z)
            def _():
                send_down(zt).wait_recv()
                part[t] = (part[t].astype(f32) + from_high[zt].astype(f32)).astype(bf16)
                send_down(zt).start()

    @pl.loop(0, n)
    def _(d):
        t = lax.rem(me + d, n)

        @pl.when(t != me)
        def _():
            copy(low_mine.at[t], low_got.at[t], low_s.at[t], low_r.at[t], t).wait_recv()

        weighted = (low_got[t].astype(f32) * own_table[pl.ds(t, 1), :]).astype(bf16)
        grad = adapter_scale * jnp.dot(weighted, cot_ref[...], preferred_element_type=f32)

        @pl.when(t == me)
        def _():
            grad_got[t] = grad.astype(bf16)

        @pl.when(t != me)
        def _():
            grad_mine[t] = grad.astype(bf16)
            send_grad(t).start()

    gin_ref[...] = jnp.zeros_like(gin_ref)

    @pl.loop(0, n)
    def _(t):
        @pl.when(t != me)
        def _():
            copy(back_mine.at[t], back_got.at[t], back_s.at[t], back_r.at[t], t).wait_recv()

        gin_ref[...] += adapter_scale * jnp.dot(
            back_got[t], hid[t], preferred_element_type=f32
        )

    gout_ref[...] = jnp.zeros_like(gout_ref)

    @pl.loop(0, n)
    def _(t):
        @pl.when(t != me)
        def _():
            copy(grad_mine.at[t], grad_got.at[t], grad_s.at[t], grad_r.at[t], t).wait_recv()

        gout_ref[...] += grad_got[t].astype(f32)

    @pl.when(z > 0)
    def _():
        send_up(z).wait_recv()

    @pl.when(z < depth - 1)
    def _():
        send_down(z).wait_recv()

    @pl.when(z == 0)
    def _():
        comb_ref[...] = (part[me].astype(f32) + from_high[z].astype(f32)).astype(bf16)

    @pl.when(z == depth - 1)
    def _():
        comb_ref[...] = (part[me].astype(f32) + from_low[z].astype(f32)).astype(bf16)

    @pl.when((z > 0) & (z < depth - 1))
    def _():
        comb_ref[...] = (
            part[me].astype(f32) + from_low[z].astype(f32) + from_high[z].astype(f32)
        ).astype(bf16)

    @pl.loop(0, depth)
    def _(zt):
        forward(zt, lambda one: one.wait_send())
        send_rows(3, zt * 4 + (1 - y) * 2 + c, core_mate).wait_send()
        send_core(zt, 0).wait_send()
        send_core(zt, 1).wait_send()
        send_y(zt).wait_send()

        @pl.when(zt != z)
        def _():
            copy(part.at[zt], from_low.at[zt], z_s.at[zt], zu_r.at[zt], y_mate).wait_send()

    @pl.loop(1, n)
    def _(d):
        t = lax.rem(me + d, n)
        send_table(d).wait_send()
        send_low(t).wait_send()
        send_back(t).wait_send()
        send_grad(t).wait_send()


def layer(x, cot, table, cap, gate, up, down, in_b, out_b):
    n = table.shape[0]
    tok, width = cot.shape
    rank, units = in_b.shape
    vmem = pl.BlockSpec(memory_space=pltpu.VMEM)
    bf16 = jnp.bfloat16
    dma = pltpu.SemaphoreType.DMA
    return pl.pallas_call(
        layer_kernel,
        out_shape=(
            jax.ShapeDtypeStruct((tok, width), bf16),
            jax.ShapeDtypeStruct((rank, units), jnp.float32),
            jax.ShapeDtypeStruct((rank, width), jnp.float32),
        ),
        in_specs=[vmem] * 9,
        out_specs=(vmem, vmem, vmem),
        scratch_shapes=[
            pltpu.VMEM((n, tok + rank, width), bf16),
            pltpu.VMEM((n, tok, width), bf16),
            pltpu.VMEM((n // 2, tok, width), bf16),
            pltpu.VMEM((n // 4, tok, width), bf16),
            pltpu.VMEM((n // 4, tok, width), bf16),
            pltpu.VMEM((n // 4, tok, width), bf16),
            pltpu.VMEM((n, tok, units), bf16),
            pltpu.VMEM((n, n, tok), jnp.float32),
            pltpu.VMEM((n, rank, tok), bf16),
            pltpu.VMEM((n, rank, tok), bf16),
            pltpu.VMEM((n, rank, tok), bf16),
            pltpu.VMEM((n, rank, tok), bf16),
            pltpu.VMEM((n, rank, width), bf16),
            pltpu.VMEM((n, rank, width), bf16),
            dma((4, n)),
            dma((n,)),
            dma((n // 2,)),
            dma((n // 2,)),
            dma((n // 4,)),
            dma((n // 4,)),
            dma((n // 4,)),
            dma((n // 4,)),
            dma((n // 4,)),
        ]
        + [dma((n,))] * 8,
        compiler_params=pltpu.CompilerParams(
            collective_id=0, has_side_effects=True, vmem_limit_bytes=60 * 1024 * 1024
        ),
        cost_estimate=pl.CostEstimate(
            flops=20_000_000_000, bytes_accessed=30_000_000, transcendentals=0
        ),
    )(x, cot, table, cap, gate, up, down, in_b, out_b)


def per_device(
    tokens,
    cotangent,
    routes,
    router_pair_weight,
    capacity,
    training_step_index,
    frozen_gate_matrix,
    frozen_up_matrix,
    frozen_down_matrix,
    adapter_input_factor,
    adapter_output_factor,
    input_first_moment,
    output_first_moment,
    input_second_moment,
    output_second_moment,
):
    devices = lax.axis_size("exp")
    assert frozen_gate_matrix.shape[0] == 1 and devices == 16
    own_grads = cotangent[0]
    in_b = adapter_input_factor[0, 0].astype(jnp.bfloat16)
    out_b = adapter_output_factor[0, 0].astype(jnp.bfloat16)

    hits = routes[0][None, :, :] == jnp.arange(devices, dtype=jnp.int32)[:, None, None]
    table = jnp.sum(
        jnp.where(hits, router_pair_weight[0].astype(jnp.float32)[None], 0.0), axis=2
    )
    combined, grad_in, grad_out = layer(
        tokens[0],
        own_grads,
        table,
        capacity.astype(jnp.float32)[:, None],
        frozen_gate_matrix[0],
        frozen_up_matrix[0],
        frozen_down_matrix[0],
        in_b,
        out_b,
    )
    combined = combined[None]

    levels = lax.axis_size("rep").bit_length() - 1
    joined_rows = jnp.concatenate((adapter_input_factor[0], adapter_output_factor[0]), axis=2)
    branches = [partial(swap_with, level_bit=level_value) for level_value in range(levels)]
    gossip_neighbor = lax.switch(training_step_index[0] % levels, branches, joined_rows)
    units = adapter_input_factor.shape[3]
    mean_in = 0.5 * (adapter_input_factor[0] + gossip_neighbor[:, :, :units])
    mean_out = 0.5 * (adapter_output_factor[0] + gossip_neighbor[:, :, units:])
    power = (training_step_index[0] + 1).astype(jnp.float32)
    fix_one = 1.0 - jnp.power(jnp.float32(beta_one), power)
    fix_two = 1.0 - jnp.power(jnp.float32(beta_two), power)
    new_in, new_first_in, new_second_in = adam_update(
        mean_in, grad_in[None], input_first_moment[0], input_second_moment[0], fix_one, fix_two
    )
    new_out, new_first_out, new_second_out = adam_update(
        mean_out, grad_out[None], output_first_moment[0], output_second_moment[0], fix_one, fix_two
    )
    return (
        combined,
        new_in[None],
        new_out[None],
        new_first_in[None],
        new_first_out[None],
        new_second_in[None],
        new_second_out[None],
    )


def solution(mesh):
    placed = (
        P("rep", "exp", None),
        P("rep", "exp", None),
        P("rep", "exp", None),
        P("rep", "exp", None),
        P(),
        P(),
        P("exp", None, None),
        P("exp", None, None),
        P("exp", None, None),
        P("rep", "exp", None, None),
        P("rep", "exp", None, None),
        P("rep", "exp", None, None),
        P("rep", "exp", None, None),
        P("rep", "exp", None, None),
        P("rep", "exp", None, None),
    )
    return jax.shard_map(
        per_device,
        mesh=mesh,
        in_specs=placed,
        out_specs=(
            P("rep", "exp", None),
            P("rep", "exp", None, None),
            P("rep", "exp", None, None),
            P("rep", "exp", None, None),
            P("rep", "exp", None, None),
            P("rep", "exp", None, None),
            P("rep", "exp", None, None),
        ),
        check_vma=False,
    )
```
